32 devices in a mesh: section: 2 (over core), expert: 16 (over z, y, x).
Axes of the slice: x: 2, y: 2, z: 4, core: 2. Of those that a mesh axis runs over, the one named last changes fastest.
Arguments:
- block_input: bfloat16 [2, 8192, 768], P(None, 'expert'), may hold values from -6 to 6
- cotangent: bfloat16 [2, 8192, 768], P(None, 'expert'), may hold values from -6 to 6
- expert_ids: int32 [2, 2, 8192, 2], P(None, None, 'expert'), may hold values from 0 to 15, all different within a row; in each aligned block of 512 rows (0 to 511, 512 to 1023, ..., all dimensions but the last counted through in order) at most 68 rows name the same one
- qkv_weight: bfloat16 [2, 768, 2304], P('section'), may hold values from -0.21875 to 0.21875
- query_bias: float32 [2, 768], P('section'), may hold values from -4 to 4
- value_bias: float32 [2, 768], P('section'), may hold values from -1.5 to 1.5
- proj_weight: bfloat16 [2, 768, 768], P('section'), may hold values from -1.75 to 1.75
- proj_bias: float32 [2, 768], P('section'), may hold values from -4 to 4
- attn_gain: float32 [2, 768], P('section'), may hold values from 0.25 to 1.75
- ffn_gain: float32 [2, 768], P('section'), may hold values from 0.25 to 1.75
- router_weight: bfloat16 [2, 768, 16], P('section'), may hold values from -0.4375 to 0.4375
- in_weight: bfloat16 [2, 16, 768, 3072], P('section', 'expert'), may hold values from -0.21875 to 0.21875
- out_weight: bfloat16 [2, 16, 3072, 768], P('section', 'expert'), may hold values from -0.109375 to 0.109375
Outputs:
- section_out: bfloat16 [2, 2, 8192, 768], P('section', None, 'expert')
- section_grad: float32 [2, 2, 8192, 768], P('section', None, 'expert')
- grad_qkv: float32 [2, 768, 2304], P('section')
- grad_qbias: float32 [2, 768], P('section')
- grad_vbias: float32 [2, 768], P('section')
- grad_proj: float32 [2, 768, 768], P('section')
- grad_pbias: float32 [2, 768], P('section')
- grad_attngain: float32 [2, 768], P('section')
- grad_ffngain: float32 [2, 768], P('section')
- grad_router: float32 [2, 768, 16], P('section')
- grad_win: bfloat16 [2, 16, 768, 3072], P('section', 'expert')
- grad_wout: bfloat16 [2, 16, 3072, 768], P('section', 'expert')
The draws below stay inside these ranges and needn't reach their ends.
Inputs may be any that keep to these rules, and one draw needn't show every extreme that they name: `expert_ids`: A token's 2 ids differ. For each layer and micro-batch, among the choices of the 512 tokens of one device, no expert is named more than 68 times, a bound that some block reaches.
All inputs are finite; a program needn't handle non-finite values.
Results may differ from the reference program's by a relative error of at most 0.02.
Values may be sent and summed in bfloat16 or wider, within the bound.
A program may use at most 384 MiB of HBM per device.

```python
import math
import jax
import jax.numpy as jnp
import numpy as np
from jax import lax

D = 768
H = 12
HD = 64
FF = 3072
TOP = 2
SEQ = 512
MICRO = 2
TOK_DEV = 512
EXPERTS = 16
TOKENS = 8192
CAP = 68
N_EXPERT = 16


def shard_levels(key, shape, split, low, top_value):
    factor_of, own = 1.0, jax.random.fold_in(key, 6)
    for position, shards_of in split:
        heights = jnp.exp(jax.random.uniform(jax.random.fold_in(own, position), (shards_of,), jnp.float32, low / len(split), top_value / len(split)))
        factor_of = factor_of * jnp.repeat(heights, shape[position] // shards_of).reshape([-1 if axis == position else 1 for axis in range(len(shape))])
    return factor_of


def deal_out(stream_key, own, number, rows, amount, top, limit, lean):
    order = jax.random.permutation(stream_key, amount)
    heavy_load, common = load_shares(amount, rows * top, limit, lean, True), load_shares(amount, rows * top, limit, lean, False)
    places = jnp.arange(amount)

    def named(lengths, rotation):
        used = int((lengths > 0).sum())
        fixed = max(1, used // 4)
        shifted = fixed + (places - fixed + rotation * (used - fixed)) % max(1, amount - fixed)
        return jnp.zeros((amount,), jnp.int32).at[order[jnp.where(places < fixed, places, shifted)]].set(jnp.asarray(lengths, jnp.int32))

    lengths = jnp.where(number % 4 == 0, named(heavy_load, number // 4), named(common, number - number // 4 - 1))
    mixed = jax.random.permutation(jax.random.fold_in(own, 3), amount)
    donor, sink = mixed[0:amount // 2 * 2:2], mixed[1:amount // 2 * 2:2]
    room = jnp.minimum(lengths[donor] - 1, limit - lengths[sink]) // 2
    room = jnp.where((donor == order[0]) | (sink == order[0]) | (lengths[sink] == 0), 0, jnp.maximum(room, 0))
    shifted = jax.random.randint(jax.random.fold_in(own, 4), (amount // 2,), 0, 1 << 20) % (room + 1)
    lengths = lengths.at[donor].add(-shifted).at[sink].add(shifted)
    items = jnp.searchsorted(jnp.cumsum(lengths), jnp.arange(rows * top), side="right").astype(jnp.int32)
    table = items.reshape(top, rows).T
    table = table[jax.random.permutation(jax.random.fold_in(own, 1), rows)]
    rotation = jax.random.randint(jax.random.fold_in(own, 2), (rows, 1), 0, top)
    return jnp.take_along_axis(table, (jnp.arange(top)[None, :] + rotation) % top, axis=1)


def load_shares(count, total, limit, slope, full):
    weights = [(1 << 20) // math.isqrt(grade ** slope) + 1 for grade in range(1, count + 1)]
    largest = limit if full else min(limit, max(-(-total // count), total * weights[0] // sum(weights)))
    least = 1 if total - largest >= count - 1 else 0
    given, surplus = [largest] + [least] * (count - 1), total - largest - least * (count - 1)
    while surplus > 0:
        movable = [i for i in range(1, count) if given[i] < largest] or [i for i in range(1, count) if given[i] < limit]
        pool, budget = sum([weights[i] for i in movable]), surplus
        for i in movable:
            more = min(limit - given[i], max(1, budget * weights[i] // pool), surplus)
            given[i] = given[i] + more
            surplus = surplus - more
    return np.array(given)


def scatter_about(own_key, extent, deviation, reach, pieces=(), held_as=jnp.bfloat16):
    drawn = jax.random.normal(own_key, extent, jnp.float32) * deviation
    if len(pieces) > 0:
        drawn = shard_levels(own_key, extent, pieces, -0.22, 0.18) * drawn
    return jnp.clip(drawn, min=-reach, max=reach).astype(held_as)


def setup_inputs(seed: int = 0) -> dict:
    splits = jax.random.split(jax.random.key(seed), 14)
    block_input = scatter_about(splits[0], (MICRO, TOKENS, D), 1.0, 6.0, ((1, 16),))
    cotangent = scatter_about(splits[1], (MICRO, TOKENS, D), 1.0, 6.0, ((1, 16),))
    expert_ids_keys = jax.random.split(jax.random.fold_in(splits[2], 1), 2 * MICRO * TOKENS // TOK_DEV)
    expert_ids_turns = jax.random.permutation(jax.random.fold_in(splits[2], 3), 2 * MICRO * TOKENS // TOK_DEV)
    expert_ids = jax.vmap(lambda own, number: deal_out(jax.random.fold_in(splits[2], 2), own, number, TOK_DEV, EXPERTS, TOP, CAP, 2))(expert_ids_keys, expert_ids_turns).reshape((2, MICRO, TOKENS, TOP))
    qkv_weight = scatter_about(splits[3], (2, D, 3 * D), D ** -0.5, 0.21875, ((0, 2),))
    query_bias = scatter_about(splits[4], (2, D), 0.3, 4.0, ((0, 2),), jnp.float32)
    value_bias = scatter_about(splits[5], (2, D), 0.1, 1.5, ((0, 2),), jnp.float32)
    proj_weight = scatter_about(splits[6], (2, D, D), (D // 64) ** -0.5, 1.75, ((0, 2),))
    proj_bias = scatter_about(splits[7], (2, D), 0.3, 4.0, ((0, 2),), jnp.float32)
    attn_gain = jnp.clip(1.0 + 0.15 * jax.random.normal(splits[8], (2, D), jnp.float32), 0.25, 1.75)
    ffn_gain = jnp.clip(1.0 + 0.15 * jax.random.normal(splits[9], (2, D), jnp.float32), 0.25, 1.75)
    router_weight = scatter_about(splits[10], (2, D, EXPERTS), (D // 4) ** -0.5, 0.4375, ((0, 2),))
    in_weight = scatter_about(splits[11], (2, EXPERTS, D, FF), D ** -0.5, 0.21875, ((0, 2), (1, 16)))
    out_weight = scatter_about(splits[12], (2, EXPERTS, FF, D), FF ** -0.5, 0.109375, ((0, 2), (1, 16)))
    return dict(block_input=block_input, cotangent=cotangent, expert_ids=expert_ids, qkv_weight=qkv_weight, query_bias=query_bias, value_bias=value_bias, proj_weight=proj_weight, proj_bias=proj_bias, attn_gain=attn_gain, ffn_gain=ffn_gain, router_weight=router_weight, in_weight=in_weight, out_weight=out_weight)


HIGH = lax.Precision.HIGHEST
EPS = 1e-06
NEG = -1e+30

@jax.custom_vjp
def low(v):
    return lax.optimization_barrier(v.astype(jnp.bfloat16)).astype(jnp.float32)

@jax.custom_vjp
def low_back(v):
    return v

def reduced_precision_saved(v):
    return (low(v), None)

def low_pass(kept, grad):
    return (grad,)

def back_keep(v):
    return (v, None)

def back_low(kept, grad):
    return (low(grad),)
low.defvjp(reduced_precision_saved, low_pass)
low_back.defvjp(back_keep, back_low)

def norm_apply(field, scaling):
    return field * lax.rsqrt(lax.optimization_barrier(jnp.mean(field * field, axis=-1, keepdims=True)) + EPS) * scaling

def router_gates(logits, choose):
    probs_all = jax.nn.softmax(logits, axis=-1)
    picked = lax.optimization_barrier(jnp.sum(probs_all[:, None, :] * choose, axis=-1))
    return picked / lax.optimization_barrier(jnp.sum(picked, axis=-1, keepdims=True))

def attend_one(queries, key_rows, value_rows):
    scores = jnp.einsum('qhd,khd->hqk', queries, key_rows, precision=HIGH) * HD ** (-0.5)
    scores = low_back(scores)
    length = scores.shape[-1]
    causal = jnp.arange(length)[:, None] >= jnp.arange(length)[None, :]
    scores = jnp.where(causal[None], scores, NEG)
    weights = low(jax.nn.softmax(scores, axis=-1))
    return jnp.einsum('hqk,khd->qhd', weights, value_rows, precision=HIGH)

def expert_layer(routed, route_ids, gating, in_weight, out_weight):
    blocks = N_EXPERT
    per_block = routed.shape[0] // blocks
    flat_ids = route_ids.reshape(blocks, per_block * TOP)
    marked = (flat_ids[:, :, None] == jnp.arange(EXPERTS, dtype=jnp.int32)[None, None, :]).astype(jnp.int32)
    ranked = lax.optimization_barrier(jnp.sum(jnp.cumsum(marked, axis=1) * marked, axis=-1)) - 1
    slot_ids = (flat_ids * CAP + ranked).astype(jnp.int32)
    lane_ids = jnp.repeat(jnp.arange(blocks, dtype=jnp.int32)[:, None], per_block * TOP, axis=1)
    copies = low_back(jnp.repeat(routed.reshape(blocks, per_block, D), TOP, axis=1))
    buffer = jnp.zeros((blocks, EXPERTS * CAP, D), jnp.float32).at[lane_ids, slot_ids].set(copies)
    buffer = buffer.reshape(blocks, EXPERTS, CAP, D)
    hidden = low_back(jnp.einsum('necd,edf->necf', buffer, in_weight, precision=HIGH))
    active = low(jax.nn.gelu(hidden))
    result = low_back(low(jnp.einsum('necf,efd->necd', active, out_weight, precision=HIGH)))
    picked = result.reshape(blocks, EXPERTS * CAP, D)[lane_ids, slot_ids]
    picked = picked.reshape(blocks * per_block, TOP, D)
    return lax.optimization_barrier(jnp.sum(gating[:, :, None] * picked, axis=1))

def layer_apply(params, route_ids, inputs):
    qkv_w, qbias, vbias, proj_w, pbias, gain_attn, gain_ffn, router_w, win_all, wout_all = params
    tokens = inputs.shape[0]
    normed = low(norm_apply(inputs, gain_attn))
    packed = jnp.dot(normed, qkv_w, precision=HIGH)
    queries = low_back(low(packed[:, :D] + qbias))
    key_rows = low_back(low(packed[:, D:2 * D]))
    value_rows = low_back(low(packed[:, 2 * D:] + vbias))
    grid_shape = (tokens // SEQ, SEQ, H, HD)
    attended = lax.map(lambda trio: jax.checkpoint(attend_one)(*trio), (queries.reshape(grid_shape), key_rows.reshape(grid_shape), value_rows.reshape(grid_shape)))
    attended = low_back(low(attended.reshape(tokens, D)))
    branch = low_back(jnp.dot(attended, proj_w, precision=HIGH) + pbias)
    between_sections = inputs + branch
    routed = low(norm_apply(between_sections, gain_ffn))
    logits = jnp.dot(routed, router_w, precision=HIGH)
    choose = (route_ids[:, :, None] == jnp.arange(EXPERTS, dtype=jnp.int32)[None, None, :]).astype(jnp.float32)
    gating = router_gates(logits, choose)
    mixture = expert_layer(routed, route_ids, gating, win_all, wout_all)
    return between_sections + mixture

def reference(block_input, cotangent, expert_ids, qkv_weight, query_bias, value_bias, proj_weight, proj_bias, attn_gain, ffn_gain, router_weight, in_weight, out_weight):
    params = tuple((weight_set.astype(jnp.float32) for weight_set in (qkv_weight, query_bias, value_bias, proj_weight, proj_bias, attn_gain, ffn_gain, router_weight, in_weight, out_weight)))
    firsts = []
    seconds = []
    grads_in = []
    grads_mid = []
    totals = None
    for step_index in range(MICRO):

        def forward(weight_sets, inputs, probe_zero):
            first_out = layer_apply(tuple((weight_set[0] for weight_set in weight_sets)), expert_ids[0, step_index], inputs)
            handed = low(first_out)
            second = layer_apply(tuple((weight_set[1] for weight_set in weight_sets)), expert_ids[1, step_index], low_back(handed + probe_zero))
            return (second, handed)
        inputs = block_input[step_index].astype(jnp.float32)
        second, pullback, handed = jax.vjp(forward, params, inputs, jnp.zeros_like(inputs), has_aux=True)
        grad_params, grad_inputs, grad_probe = pullback(cotangent[step_index].astype(jnp.float32))
        if totals is None:
            totals = grad_params
        else:
            totals = jax.tree.map(jnp.add, totals, grad_params)
        firsts.append(handed)
        seconds.append(second)
        grads_in.append(grad_inputs)
        grads_mid.append(grad_probe)
    section_out = jnp.stack([jnp.stack(firsts), jnp.stack(seconds)]).astype(jnp.bfloat16)
    section_grad = jnp.stack([jnp.stack(grads_in), jnp.stack(grads_mid)])
    return (section_out, section_grad, totals[0], totals[1], totals[2], totals[3], totals[4], totals[5], totals[6], totals[7], totals[8].astype(jnp.bfloat16), totals[9].astype(jnp.bfloat16))
```

```python
import jax
import jax.numpy as jnp
from jax import lax
from jax.sharding import PartitionSpec as P

HD = 64
EPS = 1e-06
NEG = -1e30
BF = jnp.bfloat16
F32 = jnp.float32
HIGH = lax.Precision.HIGHEST
SWAP = [(0, 1), (1, 0)]


def dot(a, b, dims, kind=F32, precision=None):
    return lax.dot_general(
        a, b, (dims, ((), ())), precision=precision, preferred_element_type=F32
    ).astype(kind)


NN = ((1,), (0,))
NT = ((1,), (1,))
TN = ((0,), (0,))


def capacity_of(tokens, choices, experts):
    return tokens * choices // experts + max(1, tokens * choices // (16 * experts))


def inverse_rms(field):
    return lax.rsqrt(jnp.mean(field * field, axis=-1, keepdims=True) + EPS)


def norm_back(field, gain, grad):
    scale = inverse_rms(field)
    unit = field * scale
    grad_gain = jnp.sum(grad * unit, axis=0)
    scaled = grad * gain
    grad_field = scale * (scaled - unit * jnp.mean(scaled * unit, axis=-1, keepdims=True))
    return grad_field, grad_gain


def causal_scores(queries, key_rows):
    scores = jnp.einsum(
        "qhd,khd->hqk", queries, key_rows, preferred_element_type=F32
    ) * HD ** (-0.5)
    length = scores.shape[-1]
    causal = jnp.arange(length)[:, None] >= jnp.arange(length)[None, :]
    return jnp.where(causal[None], scores, NEG)


def attend_forward(queries, key_rows, value_rows):
    tokens, width = queries.shape
    shape = (tokens, width // HD, HD)
    scores = causal_scores(queries.reshape(shape), key_rows.reshape(shape))
    row_max = jnp.max(scores, axis=-1, keepdims=True)
    weights = jnp.exp(scores - row_max)
    row_total = jnp.sum(weights, axis=-1, keepdims=True)
    prob_low = (weights / row_total).astype(BF)
    attended = jnp.einsum(
        "hqk,khd->qhd", prob_low, value_rows.reshape(shape), preferred_element_type=F32
    )
    return (
        attended.astype(BF).reshape(tokens, width),
        row_max[..., 0] + jnp.log(row_total[..., 0]),
    )


def attend_backward(queries, key_rows, value_rows, log_total, grad_out):
    tokens, width = queries.shape
    shape = (tokens, width // HD, HD)
    queries, key_rows, value_rows, grad_out = (
        part.reshape(shape) for part in (queries, key_rows, value_rows, grad_out)
    )
    scores = causal_scores(queries, key_rows)
    weights = jnp.exp(scores - log_total[..., None])
    grad_probs = jnp.einsum("qhd,khd->hqk", grad_out, value_rows, preferred_element_type=F32)
    inner = jnp.sum(weights * grad_probs, axis=-1, keepdims=True)
    grad_scores = (weights * (grad_probs - inner)).astype(BF)
    grad_value = jnp.einsum(
        "hqk,qhd->khd", weights.astype(BF), grad_out, preferred_element_type=F32
    )
    grad_query = jnp.einsum(
        "hqk,khd->qhd", grad_scores, key_rows, preferred_element_type=F32
    ) * HD ** (-0.5)
    grad_key = jnp.einsum(
        "hqk,qhd->khd", grad_scores, queries, preferred_element_type=F32
    ) * HD ** (-0.5)
    return tuple(
        part.astype(BF).reshape(tokens, width) for part in (grad_query, grad_key, grad_value)
    )


def gelu_and_slope(hidden):
    root = 0.7978845608028654
    square = hidden * hidden
    bent = jnp.tanh(root * hidden * (1.0 + 0.044715 * square))
    half = 0.5 * (1.0 + bent)
    slope = half + 0.5 * hidden * (1.0 - bent * bent) * root * (1.0 + 0.134145 * square)
    return hidden * half, slope


def route_plan(route_ids, experts, capacity):
    tokens = route_ids.shape[0]
    lanes = jnp.arange(experts, dtype=jnp.int32)[None, :]
    first = (route_ids[:, 0:1] == lanes).astype(F32)
    second = (route_ids[:, 1:2] == lanes).astype(F32)
    places = jnp.arange(tokens, dtype=jnp.int32)
    earlier = (places[:, None] > places[None, :]).astype(BF)
    counts = dot(earlier, (first + second).astype(BF), NN)
    ranks = [jnp.sum(counts * hot, axis=-1).astype(jnp.int32) for hot in (first, second)]
    slots = [route_ids[:, j] * capacity + ranks[j] for j in range(2)]
    row = jnp.arange(experts * capacity, dtype=jnp.int32)[:, None]
    place = [(row == slot[None, :]).astype(BF) for slot in slots]
    return first, second, place[0], place[1]


def exchange(rows, experts):
    total, width = rows.shape
    moved = lax.all_to_all(
        rows.reshape(experts, total // experts, width),
        "expert",
        split_axis=0,
        concat_axis=0,
        tiled=True,
    )
    return moved.reshape(total, width)


def layer_forward(current, plan, weights):
    qkv, qbias, vbias, proj, pbias, gain_attn, gain_ffn, router, win, wout = weights
    first, second, place0, place1 = plan
    width = current.shape[1]
    experts = router.shape[1]
    normed = (current * inverse_rms(current) * gain_attn).astype(BF)
    packed = dot(normed, qkv, NN)
    queries = (packed[:, :width] + qbias).astype(BF)
    key_rows = packed[:, width : 2 * width].astype(BF)
    value_rows = (packed[:, 2 * width :] + vbias).astype(BF)
    attended, log_total = attend_forward(queries, key_rows, value_rows)
    middle = current + (dot(attended, proj, NN) + pbias)
    routed = (middle * inverse_rms(middle) * gain_ffn).astype(BF)
    logits = dot(routed, router, NN)
    gap = jnp.sum(logits * (first - second), axis=-1, keepdims=True)
    gate0, gate1 = jax.nn.sigmoid(gap), jax.nn.sigmoid(-gap)
    arrived = exchange(dot(place0 + place1, routed, NN, BF), experts)
    hidden = dot(arrived, win, NN)
    active, slope = gelu_and_slope(hidden)
    active, slope = active.astype(BF), slope.astype(BF)
    produced = dot(active, wout, NN, BF)
    returned = exchange(produced, experts)
    combined0 = dot(place0, returned, TN, BF)
    combined1 = dot(place1, returned, TN, BF)
    outputs = middle + (gate0 * combined0.astype(F32) + gate1 * combined1.astype(F32))
    kept = (
        current, normed, queries, key_rows, value_rows, log_total, attended, middle, routed,
        gate0, gate1, combined0, combined1, arrived, active, slope,
    )
    return outputs, kept


def layer_backward(seed, kept, plan, weights):
    qkv, qbias, vbias, proj, pbias, gain_attn, gain_ffn, router, win, wout = weights
    first, second, place0, place1 = plan
    (
        current, normed, queries, key_rows, value_rows, log_total, attended, middle, routed,
        gate0, gate1, combined0, combined1, arrived, active, slope,
    ) = kept
    experts = router.shape[1]
    outgoing = dot(place0, (gate0 * seed).astype(BF), NN) + dot(
        place1, (gate1 * seed).astype(BF), NN
    )
    arriving = exchange(outgoing.astype(BF), experts)
    grad_active = dot(arriving, wout, NT)
    grad_hidden = (grad_active * slope.astype(F32)).astype(BF)
    returning = exchange(dot(grad_hidden, win, NT, BF), experts)
    grad_wout = dot(active, arriving, TN, BF)
    grad_win = dot(arrived, grad_hidden, TN, BF)
    grad_gap = gate0 * gate1 * jnp.sum(
        seed * (combined0.astype(F32) - combined1.astype(F32)), axis=-1, keepdims=True
    )
    grad_logits = grad_gap * (first - second)
    grad_router = dot(grad_logits, routed.astype(F32), TN, precision=HIGH)
    grad_routed = dot(place0 + place1, returning, TN) + dot(
        grad_logits, router.astype(F32), NT, precision=HIGH
    )
    grad_middle, grad_gain_ffn = norm_back(middle, gain_ffn, grad_routed)
    grad_middle = grad_middle + seed
    grad_branch = grad_middle.astype(BF)
    grad_pbias = jnp.sum(grad_branch.astype(F32), axis=0)
    grad_proj = dot(attended, grad_branch, TN, BF)
    grad_attended = dot(grad_branch, proj, NT, BF)
    grad_query, grad_key, grad_value = attend_backward(
        queries, key_rows, value_rows, log_total, grad_attended
    )
    grad_packed = jnp.concatenate([grad_query, grad_key, grad_value], axis=1)
    grad_qbias = jnp.sum(grad_query.astype(F32), axis=0)
    grad_vbias = jnp.sum(grad_value.astype(F32), axis=0)
    grad_qkv = [dot(normed, part, TN, BF) for part in (grad_query, grad_key, grad_value)]
    grad_normed = dot(grad_packed, qkv, NT)
    grad_current, grad_gain_attn = norm_back(current, gain_attn, grad_normed)
    grad_current = grad_current + grad_middle
    small = jnp.concatenate(
        [
            jnp.stack([grad_qbias, grad_vbias, grad_pbias, grad_gain_attn, grad_gain_ffn]),
            grad_router,
        ]
    )
    small = jnp.pad(small, ((0, -small.shape[0] % 32), (0, 0)))
    shared = jnp.concatenate(grad_qkv + [grad_proj, small.astype(BF)])
    return grad_current, shared, grad_win, grad_wout


def reduce_shared(shared, section):
    half = shared.shape[0] // 2
    own = lax.dynamic_slice_in_dim(shared, section * half, half, 0)
    other = lax.dynamic_slice_in_dim(shared, (1 - section) * half, half, 0)
    other = lax.ppermute(other, "section", SWAP)
    return lax.psum((own.astype(F32) + other.astype(F32)).astype(BF), "expert")


def both(own, other, is_first):
    return jnp.where(is_first, own, other), jnp.where(is_first, other, own)


def shards(
    block_input, cotangent, expert_ids, qkv_weight, query_bias, value_bias, proj_weight,
    proj_bias, attn_gain, ffn_gain, router_weight, in_weight, out_weight,
):
    section = lax.axis_index("section")
    is_first = section == 0
    width = block_input.shape[2]
    experts = router_weight.shape[2]
    tokens = block_input.shape[1]
    capacity = capacity_of(tokens, expert_ids.shape[3], experts)

    def gathered(array):
        return lax.all_gather(array, "section", axis=0, tiled=True)

    vectors = gathered(
        jnp.stack([query_bias, value_bias, proj_bias, attn_gain, ffn_gain], axis=1)
    )
    qkv_all, proj_all, router_all = (
        gathered(part) for part in (qkv_weight, proj_weight, router_weight)
    )
    win_all, wout_all = gathered(in_weight), gathered(out_weight)
    layers = [
        (
            qkv_all[l], vectors[l, 0], vectors[l, 1], proj_all[l], vectors[l, 2], vectors[l, 3],
            vectors[l, 4], router_all[l], win_all[l, 0], wout_all[l, 0],
        )
        for l in range(2)
    ]
    rows = lax.dynamic_index_in_dim(block_input, section, 0, keepdims=False)
    seed = lax.dynamic_index_in_dim(cotangent, section, 0, keepdims=False)
    ids = lax.dynamic_index_in_dim(expert_ids, section, 1, keepdims=False)
    plans = [route_plan(ids[l], experts, capacity) for l in range(2)]

    out0, kept0 = layer_forward(rows.astype(F32), plans[0], layers[0])
    out0 = out0.astype(BF)
    out1, kept1 = layer_forward(out0.astype(F32), plans[1], layers[1])
    out1 = out1.astype(BF)
    out_other = lax.ppermute(jnp.where(is_first, out1, out0), "section", SWAP)
    section_out = jnp.stack(both(jnp.where(is_first, out0, out1), out_other, is_first))

    grad1, shared1, win1, wout1 = layer_backward(seed.astype(F32), kept1, plans[1], layers[1])
    grad1 = grad1.astype(BF)
    up, down = [(0, 1)], [(1, 0)]
    win1_other = lax.ppermute(win1, "section", up)
    wout1_other = lax.ppermute(wout1, "section", up)
    grad1_other = lax.ppermute(grad1, "section", up)
    total1 = reduce_shared(shared1, section)
    total1_other = lax.ppermute(total1, "section", up)

    grad0, shared0, win0, wout0 = layer_backward(grad1.astype(F32), kept0, plans[0], layers[0])
    win0_other = lax.ppermute(win0, "section", down)
    wout0_other = lax.ppermute(wout0, "section", down)
    grad0_other = lax.ppermute(grad0, "section", down)
    shared0, total1 = lax.optimization_barrier((shared0, total1))
    total0 = reduce_shared(shared0, section)
    total0_other = lax.ppermute(total0, "section", down)

    section_grad = jnp.stack(
        [
            jnp.where(is_first, grad0, grad1_other.astype(F32)),
            jnp.where(is_first, grad0_other, grad1.astype(F32)),
        ]
    )

    def summed(first, first_other, second, second_other):
        return jnp.where(
            is_first,
            first.astype(F32) + first_other.astype(F32),
            second.astype(F32) + second_other.astype(F32),
        ).astype(BF)

    grad_win = summed(win0, win0_other, win1, win1_other)
    grad_wout = summed(wout0, wout0_other, wout1, wout1_other)
    total = jnp.concatenate(
        [
            jnp.where(is_first, total0, total1_other),
            jnp.where(is_first, total0_other, total1),
        ]
    ).astype(F32)
    grad_qkv = jnp.concatenate([total[i * width : (i + 1) * width] for i in range(3)], axis=1)
    grad_proj = total[3 * width : 4 * width]
    small = total[4 * width : 4 * width + 5 + experts]
    return (
        section_out[None],
        section_grad[None],
        grad_qkv[None],
        small[0][None],
        small[1][None],
        grad_proj[None],
        small[2][None],
        small[3][None],
        small[4][None],
        small[5:].T[None],
        grad_win[None, None],
        grad_wout[None, None],
    )


def solution(mesh):
    vector, matrix = P("section", None), P("section", None, None)
    expert = P("section", "expert", None, None)
    rows = P("section", None, "expert", None)
    return jax.shard_map(
        shards,
        mesh=mesh,
        in_specs=(
            P(None, "expert", None),
            P(None, "expert", None),
            P(None, None, "expert", None),
            matrix, vector, vector, matrix, vector, vector, vector, matrix, expert, expert,
        ),
        out_specs=(
            rows, rows, matrix, vector, vector, matrix, vector, vector, vector, matrix,
            expert, expert,
        ),
        check_vma=False,
    )
```
